32 devices in a mesh: grp: 2 (over core), slab: 4 (over z), col: 4 (over y, x).
Axes of the slice: x: 2, y: 2, z: 4, core: 2. Of those that a mesh axis runs over, the one named last changes fastest.
Arguments:
- solution: float32 [512, 8192], P('slab', ('grp', 'col')), may hold values from -6 to 6
- residual: float32 [512, 8192], P('slab', ('grp', 'col')), may hold values from -0.6 to 0.6
- direction: float32 [512, 8192], P('slab', ('grp', 'col')), may hold values from -6 to 6
- row_taps: float32 [31], replicated, may hold values from 0.2 to 1
- col_taps: float32 [31], replicated, may hold values from 0.2 to 1
- damping: float32 [], replicated, may hold values from 0.01 to 0.05
- rho: float32 [], replicated, may hold values from 83886.08 to 251658.23
- coarse_diag: float32 [4], replicated, may hold values from 0.9 to 1.6
- coarse_coupling: float32 [4], replicated, may hold values from 0.05 to 0.2
Outputs:
- new_solution: float32 [512, 8192], P('slab', ('grp', 'col'))
- new_residual: float32 [512, 8192], P('slab', ('grp', 'col'))
- precond: float32 [512, 8192], P('slab', ('grp', 'col'))
- new_direction: float32 [512, 8192], P('slab', ('grp', 'col'))
- energy: float32 [], replicated
The draws below stay inside these ranges and needn't reach their ends.
All inputs are finite; a program needn't handle non-finite values.
Results may differ from the reference program's by a relative error of at most 0.0001.
Values sent between devices are 32-bit elements; how exact they have to be, the bound alone decides.
A program may use at most 128 MiB of HBM per device.

```python
import math
import jax
import jax.numpy as jnp
from jax import lax

TAPS = 31
SWEEPS = 3
LEVELS = 4
COARSE_SWEEPS = 4
ROWS = 512
COLS = 8192


def shard_levels(own_key, dims, shards, smallest, largest):
    loudness = 1.0
    for dim, shards_of in shards:
        steps = jax.random.uniform(jax.random.fold_in(jax.random.fold_in(own_key, 6), dim), (shards_of,), jnp.float32, smallest / len(shards), largest / len(shards))
        loudness = loudness * jnp.repeat(jnp.exp(steps), dims[dim] // shards_of).reshape((-1,) + (1,) * (len(dims) - 1 - dim))
    return loudness


def centred(key, extent, scale, bound, pieces=(), kind=jnp.bfloat16):
    entries = jax.random.normal(key, extent, jnp.float32) * scale
    if len(pieces) > 0:
        entries = shard_levels(key, extent, pieces, -0.22, 0.18) * entries
    return jnp.clip(entries, min=-bound, max=bound).astype(kind)


def setup_inputs(seed: int = 0) -> dict:
    seeds = jax.random.split(jax.random.key(seed), 10)
    return {
        "solution": centred(seeds[0], (ROWS, COLS), 1.0, 6.0, ((0, 4), (1, 8)), jnp.float32),
        "residual": centred(seeds[1], (ROWS, COLS), 0.1, 0.6, ((0, 4), (1, 8)), jnp.float32),
        "direction": centred(seeds[2], (ROWS, COLS), 1.0, 6.0, ((0, 4), (1, 8)), jnp.float32),
        "row_taps": jnp.clip(jnp.exp(jax.random.uniform(seeds[3], (TAPS,), jnp.float32, math.log(0.2), math.log(1.0))), 0.2, 1.0),
        "col_taps": jnp.clip(jnp.exp(jax.random.uniform(seeds[4], (TAPS,), jnp.float32, math.log(0.2), math.log(1.0))), 0.2, 1.0),
        "damping": jnp.clip(jnp.exp(jax.random.uniform(seeds[5], (), jnp.float32, math.log(0.01), math.log(0.05))), 0.01, 0.05),
        "rho": jnp.clip(jnp.exp(jax.random.uniform(seeds[6], (), jnp.float32, math.log(83886.08), math.log(251658.23))), 83886.08, 251658.23),
        "coarse_diag": jnp.clip(jnp.exp(jax.random.uniform(seeds[7], (LEVELS,), jnp.float32, math.log(0.9), math.log(1.6))), 0.9, 1.6),
        "coarse_coupling": jnp.clip(jax.random.uniform(seeds[8], (LEVELS,), jnp.float32, 0.05, 0.2), 0.05, 0.2),
    }


relaxation = 2.0 / 3.0


def band_matrix(taps, out_len, in_len):
    offsets = jnp.arange(in_len)[None, :] - jnp.arange(out_len)[:, None]
    onehot = (offsets[:, :, None] == jnp.arange(taps.shape[0])[None, None, :]).astype(taps.dtype)
    return jnp.einsum("ijt,t->ij", onehot, taps, precision=lax.Precision.HIGHEST)


def blur_cols(padded, taps, length):
    height = padded.shape[0]
    blocks = -(-length // 128)
    extra = blocks * 128 + 128 - padded.shape[1]
    padded = jnp.pad(padded, ((0, 0), (0, extra)))
    main = padded[:, :blocks * 128].reshape(height, blocks, 128)
    tail = padded[:, 128:blocks * 128 + 128].reshape(height, blocks, 128)[:, :, :taps.shape[0] - 1]
    window = jnp.concatenate([main, tail], axis=2)
    matrix = band_matrix(taps, 128, 128 + taps.shape[0] - 1).T
    result = jnp.einsum("rbk,kc->rbc", window, matrix, precision=lax.Precision.HIGHEST)
    return result.reshape(height, blocks * 128)[:, :length]


def blur_rows(padded, taps, length):
    matrix = band_matrix(taps, length, length + taps.shape[0] - 1)
    return jnp.dot(matrix, padded, precision=lax.Precision.HIGHEST)


def apply_operator(field, row_norm, col_norm, damping):
    reach = row_norm.shape[0] // 2
    height, width = field.shape
    section = blur_cols(jnp.pad(field, ((0, 0), (reach, reach))), col_norm, width)
    section = blur_cols(jnp.pad(section, ((0, 0), (reach, reach))), col_norm[::-1], width)
    section = blur_rows(jnp.pad(section, ((reach, reach), (0, 0))), row_norm, height)
    section = blur_rows(jnp.pad(section, ((reach, reach), (0, 0))), row_norm[::-1], height)
    return section + damping * field


def coarse_operator(field, diag_value, coupling):
    padded = jnp.pad(field, 1)
    beside_all = padded[2:, 1:-1] + padded[:-2, 1:-1] + padded[1:-1, 2:] + padded[1:-1, :-2]
    return diag_value * field - coupling * beside_all


def restrict_by(field, factor, divisor):
    height, width = field.shape
    return field.reshape(height // factor, factor, width // factor, factor).sum(axis=(1, 3)) / divisor


def prolong_by(field, factor):
    height, width = field.shape
    spread = jnp.broadcast_to(field[:, None, :, None], (height, factor, width, factor))
    return spread.reshape(height * factor, width * factor)


def cycle(rhs, level, coarse_diag, coarse_coupling):
    diag_value = coarse_diag[level]
    coupling = coarse_coupling[level]
    guess = relaxation * rhs / diag_value
    if level == LEVELS - 1:
        for sweep in range(COARSE_SWEEPS - 1):
            guess = guess + relaxation * (rhs - coarse_operator(guess, diag_value, coupling)) / diag_value
        return guess
    lower = restrict_by(rhs - coarse_operator(guess, diag_value, coupling), 2, 2.0)
    guess = guess + prolong_by(cycle(lower, level + 1, coarse_diag, coarse_coupling), 2)
    return guess + relaxation * (rhs - coarse_operator(guess, diag_value, coupling)) / diag_value


def reference(solution, residual, direction, row_taps, col_taps, damping, rho, coarse_diag, coarse_coupling):
    row_norm = row_taps / jnp.sum(row_taps)
    col_norm = col_taps / jnp.sum(col_taps)
    image = apply_operator(direction, row_norm, col_norm, damping)
    alpha = rho / jnp.sum(direction * image)
    new_solution = solution + alpha * direction
    new_residual = residual - alpha * image
    scale = relaxation / (1.0 + damping)
    smooth = scale * new_residual
    for sweep in range(SWEEPS - 1):
        smooth = smooth + scale * (new_residual - apply_operator(smooth, row_norm, col_norm, damping))
    coarse = cycle(restrict_by(new_residual, 4, 4.0), 0, coarse_diag, coarse_coupling)
    precond = smooth + prolong_by(coarse, 4)
    energy = jnp.sum(new_residual * precond)
    new_direction = precond + (energy / rho) * direction
    return new_solution, new_residual, precond, new_direction, energy
```

```python
import functools

import jax
import jax.numpy as jnp
from jax import lax
from jax.experimental import pallas as pl
from jax.experimental.pallas import tpu as pltpu
from jax.sharding import PartitionSpec as P

SWEEPS = 3
LEVELS = 4
COARSE_SWEEPS = 4
RELAX = 2.0 / 3.0
HR = 32
HC = 128
BLK = 256
MESH = pl.DeviceIdType.MESH
F32 = jnp.float32
BF16 = jnp.bfloat16
DIRS = [(0, -1), (0, 1), (-1, 0), (1, 0), (-1, -1), (-1, 1), (1, -1), (1, 1)]


def split(x):
    hi = x.astype(BF16)
    return hi, (x - hi.astype(F32)).astype(BF16)


def dot(a, b):
    return jnp.dot(a, b, preferred_element_type=F32)


def dot_left(sel, x):
    hi, lo = split(x)
    return dot(sel, hi) + dot(sel, lo)


def dot_right(x, sel):
    hi, lo = split(x)
    return dot(hi, sel) + dot(lo, sel)


def iota(shape, dim):
    return lax.broadcasted_iota(jnp.int32, shape, dim)


def select(condition, value=1.0):
    return jnp.where(condition, F32(value), F32(0.0)).astype(BF16)


def lanes(n):
    return -(-n // 128) * 128


def fold(x):
    rows, cols = x.shape
    total = x.reshape(rows // 8, 8, cols).sum(axis=0)
    out = total[:, :128]
    for b in range(1, cols // 128):
        out = out + total[:, 128 * b : 128 * b + 128]
    return out


def beside(v):
    rows, cols = v.shape
    i = iota(v.shape, 0)
    up = jnp.where(i == 0, 0.0, pltpu.roll(v, 1, 0))
    down = jnp.where(i == rows - 1, 0.0, pltpu.roll(v, rows - 1, 0))
    return up + down + pltpu.roll(v, 1, 1) + pltpu.roll(v, cols - 1, 1)


def kernel(
    sizes,
    sol_in,
    res_in,
    dir_in,
    row_taps,
    col_taps,
    damping,
    rho,
    diag,
    coupling,
    sol_out,
    res_out,
    pre_out,
    ndir_out,
    energy_out,
    fields,
    band,
    mc_hi,
    mc_lo,
    mr_hi,
    mr_lo,
    t_hi,
    t_lo,
    sum4,
    spread4,
    sol_buf,
    pre_buf,
    ndir_buf,
    rhs1,
    plane_sum,
    slab_sum,
    local_sem,
    out_sem,
    send_sem,
    recv_sem,
    gsend_sem,
    grecv_sem,
    psend_sem,
    precv_sem,
    ssend_sem,
    srecv_sem,
):
    H, W, n_slab, n_grp, n_col, taps = sizes
    n_lin = n_grp * n_col
    reach = taps // 2
    PH, PW = H + 2 * HR, W + 2 * HC
    slab = lax.axis_index("slab")
    lin = lax.axis_index("grp") * n_col + lax.axis_index("col")

    def device(s, l):
        return (l // n_col, s, l % n_col)

    def exists(dz, dc):
        s, l = slab + dz, lin + dc
        return (s >= 0) & (s < n_slab) & (l >= 0) & (l < n_lin)

    centre = (pl.ds(HR, H), pl.ds(HC, W))

    loads = [
        pltpu.make_async_copy(dir_in, fields.at[0].at[centre], local_sem.at[0]),
        pltpu.make_async_copy(res_in, fields.at[1].at[centre], local_sem.at[1]),
        pltpu.make_async_copy(sol_in, sol_buf, local_sem.at[2]),
    ]
    for load in loads:
        load.start()

    barrier = pltpu.get_barrier_semaphore()
    for i in range(1, n_lin):
        pl.semaphore_signal(
            barrier, inc=1, device_id=device(slab, (lin + i) % n_lin), device_id_type=MESH
        )
    for dc in (-1, 0, 1):

        @pl.when(exists(0, dc))
        def _():
            for i in range(1, n_slab):
                pl.semaphore_signal(
                    barrier,
                    inc=1,
                    device_id=device((slab + i) % n_slab, lin + dc),
                    device_id_type=MESH,
                )

    def side(d, halo, extent):
        return {-1: (0, halo), 0: (halo, extent), 1: (halo + extent, halo)}[d]

    for dz, dc in DIRS:
        r0, rn = side(dz, HR, H)
        c0, cn = side(dc, HC, W)

        @pl.when(jnp.logical_not(exists(dz, dc)))
        def _():
            for f in range(4):
                fields[f, r0 : r0 + rn, c0 : c0 + cn] = jnp.zeros((rn, cn), F32)

    W1 = W // 8
    H1 = H // 8
    for dc, c0 in ((-1, 0), (1, 2 * W1)):

        @pl.when(jnp.logical_not(exists(0, dc)))
        def _():
            rhs1[:, c0 : c0 + W1] = jnp.zeros((H1 * n_slab, W1), F32)

    near = 1 + (lin > 0).astype(jnp.int32) + (lin < n_lin - 1).astype(jnp.int32)
    pl.semaphore_wait(barrier, n_lin - 1 + (n_slab - 1) * near)

    def halo_copy(f, source, k):
        dz, dc = DIRS[k]

        def cut(d, halo, extent):
            src = {-1: (0, halo), 0: (0, extent), 1: (extent - halo, halo)}[d]
            dst = side(-d, halo, extent)[0]
            return src[0], dst, src[1]

        rs, rd, rn = cut(dz, HR, H)
        cs, cd, cn = cut(dc, HC, W)
        if source is None:
            src = fields.at[f, pl.ds(HR + rs, rn), pl.ds(HC + cs, cn)]
        else:
            src = source.at[pl.ds(rs, rn), pl.ds(cs, cn)]
        return pltpu.make_async_remote_copy(
            src_ref=src,
            dst_ref=fields.at[f, pl.ds(rd, rn), pl.ds(cd, cn)],
            send_sem=send_sem.at[f, k],
            recv_sem=recv_sem.at[f, k],
            device_id=device(slab + dz, lin + dc),
            device_id_type=MESH,
        )

    def halo_start(f, source=None):
        for k, (dz, dc) in enumerate(DIRS):

            @pl.when(exists(dz, dc))
            def _():
                halo_copy(f, source, k).start()

    def halo_arrive(f, source=None):
        for k, (dz, dc) in enumerate(DIRS):

            @pl.when(exists(-dz, -dc))
            def _():
                halo_copy(f, source, k).wait_recv()

    def halo_sent(f, source=None):
        for k, (dz, dc) in enumerate(DIRS):

            @pl.when(exists(dz, dc))
            def _():
                halo_copy(f, source, k).wait_send()

    halo_start(0, dir_in)
    halo_start(1, res_in)

    def banded(ref, first, rows, cols, offset):
        total = ref[0]
        for a in range(1, taps):
            total = total + ref[a]
        inverse = 1.0 / jnp.full((1, 1), total, F32)
        gap = iota((rows, cols), 1) - iota((rows, cols), 0) + (reach + offset - first)
        out = jnp.zeros((rows, cols), F32)
        for a in range(taps):
            out = jnp.where(gap == a, ref[a], out)
        return out * inverse

    def gram(c, keep):
        hi, lo = split(c)
        khi, klo = hi[:, keep], lo[:, keep]
        hit, lot = hi.T, lo.T
        return dot(hit, khi) + dot(lot, khi) + dot(hit, klo)

    for r in range(0, PH, 32):
        band[r : r + 32, 0:PH] = banded(row_taps, r, 32, PH, 0)
    m = iota((PH, PH), 0) + (slab * H - HR)
    c = jnp.where((m >= 0) & (m < H * n_slab), band[0:PH, 0:PH], 0.0)
    hi, lo = split(c)
    hit, lot = hi.T[HR : HR + H], lo.T[HR : HR + H]
    g = dot(hit, hi) + dot(lot, hi) + dot(hit, lo)
    ghi, glo = split(g)
    mr_hi[...] = ghi
    mr_lo[...] = glo

    WIN = BLK + 2 * HC
    band[...] = jnp.zeros((WIN, WIN), F32)
    for r in range(0, 128, 32):
        strip = banded(col_taps, r, 32, 384, -128)
        for b in range(WIN // 128):
            low = max(b - 1, 0)
            high = min(b + 2, WIN // 128)
            band[128 * b + r : 128 * b + r + 32, 128 * low : 128 * high] = strip[
                :, 128 * (low - b + 1) : 128 * (high - b + 1)
            ]
    blocks = W // BLK
    for v, j in ((0, 0), (1, None), (2, blocks - 1)):
        c = band[...]
        if j is not None:
            m = iota((WIN, WIN), 0) + (lin * W + BLK * j - HC)
            c = jnp.where((m >= 0) & (m < W * n_lin), c, 0.0)
        ghi, glo = split(gram(c, slice(HC, HC + BLK)))
        mc_hi[v] = ghi
        mc_lo[v] = glo

    H0, W0 = H // 4, W // 4
    PH0, PW0 = PH // 4, lanes(PW // 4)
    sum4[...] = select((iota((PW, PW0), 0) >> 2) == iota((PW, PW0), 1), 0.25)
    spread4[...] = select(
        ((iota((PW0, W), 1) + HC) >> 2) == iota((PW0, W), 0)
    )

    damp = jnp.full((1, 1), damping[0], F32)

    def apply_a(f, emit):
        for j in range(PW // BLK):
            cols = slice(BLK * j, BLK * j + BLK)
            xh, xl = split(fields[f, :, cols])
            t = dot(mr_hi[...], xh) + dot(mr_hi[...], xl) + dot(mr_lo[...], xh)
            th, tl = split(t)
            t_hi[:, cols] = th
            t_lo[:, cols] = tl
        for j in range(blocks):
            v = 0 if j == 0 else (2 if j == blocks - 1 else 1)
            win = slice(BLK * j, BLK * j + WIN)
            th, tl = t_hi[:, win], t_lo[:, win]
            mh, ml = mc_hi[v], mc_lo[v]
            x = fields[f, HR : HR + H, HC + BLK * j : HC + BLK * j + BLK]
            emit(j, x, dot(th, mh) + dot(tl, mh) + dot(th, ml) + damp * x)

    def put(f, j, value):
        fields[f, HR : HR + H, HC + BLK * j : HC + BLK * j + BLK] = value

    def plane_copy(e, i):
        return pltpu.make_async_remote_copy(
            src_ref=plane_sum.at[e, lin],
            dst_ref=plane_sum.at[e, lin],
            send_sem=psend_sem.at[e, i],
            recv_sem=precv_sem.at[e, i],
            device_id=device(slab, (lin + i) % n_lin),
            device_id_type=MESH,
        )

    def slab_copy(e, i):
        return pltpu.make_async_remote_copy(
            src_ref=slab_sum.at[e, slab],
            dst_ref=slab_sum.at[e, slab],
            send_sem=ssend_sem.at[e, i],
            recv_sem=srecv_sem.at[e, i],
            device_id=device((slab + i) % n_slab, lin),
            device_id_type=MESH,
        )

    def reduce_start(e, value):
        plane_sum[e, lin] = value
        for i in range(1, n_lin):
            plane_copy(e, i).start()

    def reduce_middle(e):
        for i in range(1, n_lin):
            plane_copy(e, i).wait_recv()
        total = plane_sum[e, 0]
        for i in range(1, n_lin):
            total = total + plane_sum[e, i]
        slab_sum[e, slab] = total
        for i in range(1, n_slab):
            slab_copy(e, i).start()

    def reduce_end(e):
        for i in range(1, n_slab):
            slab_copy(e, i).wait_recv()
        total = slab_sum[e, 0]
        for i in range(1, n_slab):
            total = total + slab_sum[e, i]
        return jnp.sum(total, axis=(0, 1), keepdims=True)

    loads[0].wait()
    halo_arrive(0, dir_in)
    parts = []

    def emit_q(j, x, y):
        put(2, j, y)
        parts.append(fold(x * y))

    apply_a(0, emit_q)
    halo_start(2)
    reduce_start(0, functools.reduce(jnp.add, parts))
    loads[1].wait()
    loads[2].wait()
    halo_arrive(1, res_in)
    reduce_middle(0)
    halo_arrive(2)
    rho_v = jnp.full((1, 1), rho[0], F32)
    alpha = rho_v / reduce_end(0)

    pick_rows = select((iota((PH0, PH), 1) >> 2) == iota((PH0, PH), 0))
    f0 = jnp.zeros((PH0, PW0), F32)
    for j in range(PW // BLK):
        cols = slice(BLK * j, BLK * j + BLK)
        r = fields[1, :, cols] - alpha * fields[2, :, cols]
        fields[1, :, cols] = r
        f0 = f0 + dot_right(dot_left(pick_rows, r), sum4[cols, :])
    res_copy = pltpu.make_async_copy(fields.at[1].at[centre], res_out, out_sem.at[0])
    res_copy.start()

    inv_diag = [RELAX / jnp.full((1, 1), diag[l], F32) for l in range(LEVELS)]

    def operator(l, v):
        return diag[l] * v - coupling[l] * beside(v)

    v0 = inv_diag[0] * f0
    t = f0 - operator(0, v0)
    rows = select((iota((H1, PH0), 1) - HR // 4) >> 1 == iota((H1, PH0), 0), 0.5)
    cols = select((iota((PW0, W1), 0) - HC // 4) >> 1 == iota((PW0, W1), 1))
    own_rows = pl.ds(pl.multiple_of(slab * H1, 8), H1)
    rhs1[own_rows, W1 : 2 * W1] = dot_right(dot_left(rows, t), cols)

    def gather_copy(dc, i):
        return pltpu.make_async_remote_copy(
            src_ref=rhs1.at[own_rows, pl.ds(W1, W1)],
            dst_ref=rhs1.at[own_rows, pl.ds(W1 - dc * W1, W1)],
            send_sem=gsend_sem.at[dc + 1, i],
            recv_sem=grecv_sem.at[dc + 1, i],
            device_id=device((slab + i) % n_slab, lin + dc),
            device_id_type=MESH,
        )

    def gather(action):
        for dc in (-1, 0, 1):
            for_recv = action == "wait_recv"

            @pl.when(exists(0, -dc if for_recv else dc))
            def _():
                for i in range(0 if dc else 1, n_slab):
                    getattr(gather_copy(dc, i), action)()

    gather("start")

    squares = []

    def emit_ar(j, x, y):
        put(3, j, y)
        squares.append((fold(x * x), fold(x * y), fold(y * y)))

    apply_a(1, emit_ar)
    halo_start(3)

    sol_buf[...] = sol_buf[...] + alpha * fields[0, HR : HR + H, HC : HC + W]
    sol_copy = pltpu.make_async_copy(sol_buf, sol_out, out_sem.at[1])
    sol_copy.start()

    gather("wait_recv")

    def level_shape(l):
        return (H1 * n_slab) >> (l - 1), lanes((3 * W1) >> (l - 1))

    def inside(l):
        shape = level_shape(l)
        width = W1 >> (l - 1)
        j = iota(shape, 1)
        column = j + (lin - 1) * width
        return (j < 3 * width) & (column >= 0) & (column < width * n_lin)

    def level(l, f):
        mask = inside(l)
        scale = inv_diag[l]
        v = scale * f
        if l == LEVELS - 1:
            for _ in range(COARSE_SWEEPS - 1):
                v = jnp.where(mask, v + scale * (f - operator(l, v)), 0.0)
            return v
        t = jnp.where(mask, f - operator(l, v), 0.0)
        (h, w), (hn, wn) = level_shape(l), level_shape(l + 1)
        down = select((iota((hn, h), 1) >> 1) == iota((hn, h), 0), 0.5)
        across = select((iota((w, wn), 0) >> 1) == iota((w, wn), 1))
        lower = level(l + 1, dot_right(dot_left(down, t), across))
        up = select((iota((h, hn), 0) >> 1) == iota((h, hn), 1))
        back = select((iota((wn, w), 1) >> 1) == iota((wn, w), 0))
        v = v + dot_left(up, dot_right(lower, back))
        return jnp.where(mask, v + scale * (f - operator(l, v)), 0.0)

    v1 = level(1, rhs1[...])
    R1, C1 = level_shape(1)
    up = select(((iota((PH0, R1), 0) + (slab * H0 - HR // 4)) >> 1) == iota((PH0, R1), 1))
    back = select(((iota((C1, PW0), 1) - HC // 4) >> 1) + W1 == iota((C1, PW0), 0))
    v0 = v0 + dot_right(dot_left(up, v1), back)
    v0 = v0 + inv_diag[0] * (f0 - operator(0, v0))
    i, j = iota((PH0, PW0), 0), iota((PH0, PW0), 1)
    own = (i >= HR // 4) & (i < HR // 4 + H0) & (j >= HC // 4) & (j < HC // 4 + W0)
    v0 = jnp.where(own, v0, 0.0)

    c = RELAX / (1.0 + damp)
    rr = functools.reduce(jnp.add, [s[0] for s in squares])
    ra = functools.reduce(jnp.add, [s[1] for s in squares])
    aa = functools.reduce(jnp.add, [s[2] for s in squares])
    reduce_start(
        1, 3.0 * c * rr - 3.0 * c * c * ra + c * c * c * aa + 4.0 * fold(f0 * v0)
    )

    up4 = select(((iota((H, PH0), 0) + HR) >> 2) == iota((H, PH0), 1))
    v0_hi, v0_lo = split(v0)
    wide_hi = dot(up4, v0_hi).astype(BF16)
    wide_lo = dot(up4, v0_lo).astype(BF16)

    halo_arrive(3)

    def emit_pre(j, x, y):
        cols = slice(BLK * j, BLK * j + BLK)
        r = fields[1, HR : HR + H, HC + BLK * j : HC + BLK * j + BLK]
        coarse = dot(wide_hi, spread4[:, cols]) + dot(wide_lo, spread4[:, cols])
        pre_buf[:, cols] = 3.0 * c * r - 3.0 * c * c * x + c * c * c * y + coarse

    apply_a(3, emit_pre)
    pre_copy = pltpu.make_async_copy(pre_buf, pre_out, out_sem.at[2])
    pre_copy.start()
    reduce_middle(1)
    energy = reduce_end(1)
    beta = energy / rho_v
    ndir_buf[...] = pre_buf[...] + beta * fields[0, HR : HR + H, HC : HC + W]
    ndir_copy = pltpu.make_async_copy(ndir_buf, ndir_out, out_sem.at[3])
    ndir_copy.start()
    energy_out[...] = energy

    halo_sent(0, dir_in)
    halo_sent(1, res_in)
    halo_sent(2)
    halo_sent(3)
    gather("wait_send")
    for e in range(2):
        for i in range(1, n_lin):
            plane_copy(e, i).wait_send()
        for i in range(1, n_slab):
            slab_copy(e, i).wait_send()
    res_copy.wait()
    sol_copy.wait()
    pre_copy.wait()
    ndir_copy.wait()


def solution(mesh):
    n_grp, n_slab, n_col = (mesh.shape[a] for a in ("grp", "slab", "col"))
    n_lin = n_grp * n_col

    def on_device(sol, res, direction, row_taps, col_taps, damping, rho, diag, coupling):
        H, W = sol.shape
        taps = row_taps.shape[0]
        PH, PW = H + 2 * HR, W + 2 * HC
        WIN = BLK + 2 * HC
        any_spec = pl.BlockSpec(memory_space=pl.ANY)
        smem = pl.BlockSpec(memory_space=pltpu.SMEM)
        vmem = pl.BlockSpec(memory_space=pltpu.VMEM)
        tile = jax.ShapeDtypeStruct((H, W), F32)
        dma = pltpu.SemaphoreType.DMA
        outs = pl.pallas_call(
            functools.partial(kernel, (H, W, n_slab, n_grp, n_col, taps)),
            out_shape=[tile] * 4 + [jax.ShapeDtypeStruct((1, 1), F32)],
            in_specs=[any_spec] * 3 + [smem] * 6,
            out_specs=[any_spec] * 4 + [vmem],
            scratch_shapes=[
                pltpu.VMEM((4, PH, PW), F32),
                pltpu.VMEM((WIN, WIN), F32),
                pltpu.VMEM((3, WIN, BLK), BF16),
                pltpu.VMEM((3, WIN, BLK), BF16),
                pltpu.VMEM((H, PH), BF16),
                pltpu.VMEM((H, PH), BF16),
                pltpu.VMEM((H, PW), BF16),
                pltpu.VMEM((H, PW), BF16),
                pltpu.VMEM((PW, lanes(PW // 4)), BF16),
                pltpu.VMEM((lanes(PW // 4), W), BF16),
                pltpu.VMEM((H, W), F32),
                pltpu.VMEM((H, W), F32),
                pltpu.VMEM((H, W), F32),
                pltpu.VMEM((H // 8 * n_slab, 3 * (W // 8)), F32),
                pltpu.VMEM((2, n_lin, 8, 128), F32),
                pltpu.VMEM((2, n_slab, 8, 128), F32),
                dma((3,)),
                dma((4,)),
                dma((4, 8)),
                dma((4, 8)),
                dma((3, n_slab)),
                dma((3, n_slab)),
                dma((2, n_lin)),
                dma((2, n_lin)),
                dma((2, n_slab)),
                dma((2, n_slab)),
            ],
            compiler_params=pltpu.CompilerParams(
                collective_id=0, has_side_effects=True, vmem_limit_bytes=48 * 1024 * 1024
            ),
        )(
            sol,
            res,
            direction,
            row_taps,
            col_taps,
            damping.reshape(1),
            rho.reshape(1),
            diag,
            coupling,
        )
        return (*outs[:4], outs[4].reshape(()))

    tile = P("slab", ("grp", "col"))
    return jax.shard_map(
        on_device,
        mesh=mesh,
        in_specs=(tile, tile, tile, P(), P(), P(), P(), P(), P()),
        out_specs=(tile, tile, tile, tile, P()),
        check_vma=False,
    )
```

```python
import functools

import jax
import jax.numpy as jnp
from jax import lax
from jax.experimental import pallas as pl
from jax.experimental.pallas import tpu as pltpu
from jax.sharding import PartitionSpec as P

SWEEPS = 3
LEVELS = 4
COARSE_SWEEPS = 4
RELAX = 2.0 / 3.0
HR = 32
HC = 128
BLK = 256
MESH = pl.DeviceIdType.MESH
F32 = jnp.float32
BF16 = jnp.bfloat16
DIRS = [(0, -1), (0, 1), (-1, 0), (1, 0), (-1, -1), (-1, 1), (1, -1), (1, 1)]


def split(x):
    hi = x.astype(BF16)
    return hi, (x - hi.astype(F32)).astype(BF16)


def dot(a, b):
    return jnp.dot(a, b, preferred_element_type=F32)


def dot_left(sel, x):
    hi, lo = split(x)
    return dot(sel, hi) + dot(sel, lo)


def dot_right(x, sel):
    hi, lo = split(x)
    return dot(hi, sel) + dot(lo, sel)


def iota(shape, dim):
    return lax.broadcasted_iota(jnp.int32, shape, dim)


def select(condition, value=1.0):
    return jnp.where(condition, F32(value), F32(0.0)).astype(BF16)


def lanes(n):
    return -(-n // 128) * 128


def fold(x):
    rows, cols = x.shape
    total = x.reshape(rows // 8, 8, cols).sum(axis=0)
    out = total[:, :128]
    for b in range(1, cols // 128):
        out = out + total[:, 128 * b : 128 * b + 128]
    return out


def beside(v):
    rows, cols = v.shape
    i = iota(v.shape, 0)
    up = jnp.where(i == 0, 0.0, pltpu.roll(v, 1, 0))
    down = jnp.where(i == rows - 1, 0.0, pltpu.roll(v, rows - 1, 0))
    return up + down + pltpu.roll(v, 1, 1) + pltpu.roll(v, cols - 1, 1)


def kernel(
    sizes,
    res_in,
    dir_in,
    row_taps,
    col_taps,
    damping,
    rho,
    diag,
    coupling,
    res_out,
    pre_out,
    alpha_out,
    energy_out,
    fields,
    band,
    mc_hi,
    mc_lo,
    mr_hi,
    mr_lo,
    t_hi,
    t_lo,
    sum4,
    spread4,
    pre_buf,
    rhs1,
    parts_in,
    local_sem,
    out_sem,
    send_sem,
    recv_sem,
    gsend_sem,
    grecv_sem,
    psend_sem,
    precv_sem,
):
    H, W, n_slab, n_grp, n_col, taps = sizes
    n_lin = n_grp * n_col
    reach = taps // 2
    PH, PW = H + 2 * HR, W + 2 * HC
    slab = lax.axis_index("slab")
    lin = lax.axis_index("grp") * n_col + lax.axis_index("col")

    def device(s, l):
        return (l // n_col, s, l % n_col)

    def exists(dz, dc):
        s, l = slab + dz, lin + dc
        return (s >= 0) & (s < n_slab) & (l >= 0) & (l < n_lin)

    centre = (pl.ds(HR, H), pl.ds(HC, W))

    loads = [
        pltpu.make_async_copy(dir_in, fields.at[0].at[centre], local_sem.at[0]),
        pltpu.make_async_copy(res_in, fields.at[1].at[centre], local_sem.at[1]),
    ]
    for load in loads:
        load.start()

    barrier = pltpu.get_barrier_semaphore()
    count = n_slab * n_lin
    me = slab * n_lin + lin

    def other(i):
        index = (me + i) % count
        return device(index // n_lin, index % n_lin)

    def greet(i, carry):
        pl.semaphore_signal(barrier, inc=1, device_id=other(i), device_id_type=MESH)
        return carry

    lax.fori_loop(1, count, greet, 0)

    def side(d, halo, extent):
        return {-1: (0, halo), 0: (halo, extent), 1: (halo + extent, halo)}[d]

    for dz, dc in DIRS:
        r0, rn = side(dz, HR, H)
        c0, cn = side(dc, HC, W)

        @pl.when(jnp.logical_not(exists(dz, dc)))
        def _():
            for f in range(4):
                fields[f, r0 : r0 + rn, c0 : c0 + cn] = jnp.zeros((rn, cn), F32)

    W1 = W // 8
    H1 = H // 8
    for dc, c0 in ((-1, 0), (1, 2 * W1)):

        @pl.when(jnp.logical_not(exists(0, dc)))
        def _():
            rhs1[:, c0 : c0 + W1] = jnp.zeros((H1 * n_slab, W1), F32)

    pl.semaphore_wait(barrier, count - 1)

    def halo_copy(f, source, k):
        dz, dc = DIRS[k]

        def cut(d, halo, extent):
            src = {-1: (0, halo), 0: (0, extent), 1: (extent - halo, halo)}[d]
            dst = side(-d, halo, extent)[0]
            return src[0], dst, src[1]

        rs, rd, rn = cut(dz, HR, H)
        cs, cd, cn = cut(dc, HC, W)
        if source is None:
            src = fields.at[f, pl.ds(HR + rs, rn), pl.ds(HC + cs, cn)]
        else:
            src = source.at[pl.ds(rs, rn), pl.ds(cs, cn)]
        return pltpu.make_async_remote_copy(
            src_ref=src,
            dst_ref=fields.at[f, pl.ds(rd, rn), pl.ds(cd, cn)],
            send_sem=send_sem.at[f, k],
            recv_sem=recv_sem.at[f, k],
            device_id=device(slab + dz, lin + dc),
            device_id_type=MESH,
        )

    def halo_start(f, source=None):
        for k, (dz, dc) in enumerate(DIRS):

            @pl.when(exists(dz, dc))
            def _():
                halo_copy(f, source, k).start()

    def halo_arrive(f, source=None):
        for k, (dz, dc) in enumerate(DIRS):

            @pl.when(exists(-dz, -dc))
            def _():
                halo_copy(f, source, k).wait_recv()

    def halo_sent(f, source=None):
        for k, (dz, dc) in enumerate(DIRS):

            @pl.when(exists(dz, dc))
            def _():
                halo_copy(f, source, k).wait_send()

    halo_start(0, dir_in)
    halo_start(1, res_in)

    def banded(ref, first, rows, cols, offset):
        total = ref[0]
        for a in range(1, taps):
            total = total + ref[a]
        inverse = 1.0 / jnp.full((1, 1), total, F32)
        gap = iota((rows, cols), 1) - iota((rows, cols), 0) + (reach + offset - first)
        out = jnp.zeros((rows, cols), F32)
        for a in range(taps):
            out = jnp.where(gap == a, ref[a], out)
        return out * inverse

    def gram(c, keep):
        hi, lo = split(c)
        khi, klo = hi[:, keep], lo[:, keep]
        hit, lot = hi.T, lo.T
        return dot(hit, khi) + dot(lot, khi) + dot(hit, klo)

    for r in range(0, PH, 32):
        band[r : r + 32, 0:PH] = banded(row_taps, r, 32, PH, 0)
    m = iota((PH, PH), 0) + (slab * H - HR)
    c = jnp.where((m >= 0) & (m < H * n_slab), band[0:PH, 0:PH], 0.0)
    hi, lo = split(c)
    hit, lot = hi.T[HR : HR + H], lo.T[HR : HR + H]
    g = dot(hit, hi) + dot(lot, hi) + dot(hit, lo)
    ghi, glo = split(g)
    mr_hi[...] = ghi
    mr_lo[...] = glo

    WIN = BLK + 2 * HC
    band[...] = jnp.zeros((WIN, WIN), F32)
    for r in range(0, 128, 32):
        strip = banded(col_taps, r, 32, 384, -128)
        for b in range(WIN // 128):
            low = max(b - 1, 0)
            high = min(b + 2, WIN // 128)
            band[128 * b + r : 128 * b + r + 32, 128 * low : 128 * high] = strip[
                :, 128 * (low - b + 1) : 128 * (high - b + 1)
            ]
    blocks = W // BLK
    for v, j in ((0, 0), (1, None), (2, blocks - 1)):
        c = band[...]
        if j is not None:
            m = iota((WIN, WIN), 0) + (lin * W + BLK * j - HC)
            c = jnp.where((m >= 0) & (m < W * n_lin), c, 0.0)
        ghi, glo = split(gram(c, slice(HC, HC + BLK)))
        mc_hi[v] = ghi
        mc_lo[v] = glo

    H0, W0 = H // 4, W // 4
    PH0, PW0 = PH // 4, lanes(PW // 4)
    sum4[...] = select((iota((PW, PW0), 0) >> 2) == iota((PW, PW0), 1), 0.25)
    spread4[...] = select(
        ((iota((PW0, W), 1) + HC) >> 2) == iota((PW0, W), 0)
    )

    damp = jnp.full((1, 1), damping[0], F32)

    def apply_a(f, emit):
        for j in range(PW // BLK):
            cols = slice(BLK * j, BLK * j + BLK)
            xh, xl = split(fields[f, :, cols])
            t = dot(mr_hi[...], xh) + dot(mr_hi[...], xl) + dot(mr_lo[...], xh)
            th, tl = split(t)
            t_hi[:, cols] = th
            t_lo[:, cols] = tl
        for j in range(blocks):
            v = 0 if j == 0 else (2 if j == blocks - 1 else 1)
            win = slice(BLK * j, BLK * j + WIN)
            th, tl = t_hi[:, win], t_lo[:, win]
            mh, ml = mc_hi[v], mc_lo[v]
            x = fields[f, HR : HR + H, HC + BLK * j : HC + BLK * j + BLK]
            emit(j, x, dot(th, mh) + dot(tl, mh) + dot(th, ml) + damp * x)

    def put(f, j, value):
        fields[f, HR : HR + H, HC + BLK * j : HC + BLK * j + BLK] = value

    def part_copy(e, i, slot):
        return pltpu.make_async_remote_copy(
            src_ref=parts_in.at[e, me],
            dst_ref=parts_in.at[e, slot],
            send_sem=psend_sem.at[e, i],
            recv_sem=precv_sem.at[e, i],
            device_id=other(i),
            device_id_type=MESH,
        )

    def each(action):
        def step(i, carry):
            action(i)
            return carry

        lax.fori_loop(1, count, step, 0)

    def reduce_start(e, value):
        parts_in[e, me] = jnp.sum(value, axis=0, keepdims=True)
        each(lambda i: part_copy(e, i, me).start())

    def reduce_end(e):
        each(lambda i: part_copy(e, i, me).wait_recv())
        return jnp.sum(jnp.sum(parts_in[e], axis=0), axis=1, keepdims=True)

    loads[0].wait()
    halo_arrive(0, dir_in)
    parts = []

    def emit_q(j, x, y):
        put(2, j, y)
        parts.append(fold(x * y))

    apply_a(0, emit_q)
    reduce_start(0, functools.reduce(jnp.add, parts))
    halo_start(2)
    loads[1].wait()
    halo_arrive(1, res_in)
    halo_arrive(2)
    rho_v = jnp.full((1, 1), rho[0], F32)
    alpha = rho_v / reduce_end(0)

    pick_rows = select((iota((PH0, PH), 1) >> 2) == iota((PH0, PH), 0))
    f0 = jnp.zeros((PH0, PW0), F32)
    for j in range(PW // BLK):
        cols = slice(BLK * j, BLK * j + BLK)
        r = fields[1, :, cols] - alpha * fields[2, :, cols]
        fields[1, :, cols] = r
        f0 = f0 + dot_right(dot_left(pick_rows, r), sum4[cols, :])
    res_copy = pltpu.make_async_copy(fields.at[1].at[centre], res_out, out_sem.at[0])
    res_copy.start()

    inv_diag = [RELAX / jnp.full((1, 1), diag[l], F32) for l in range(LEVELS)]

    def operator(l, v):
        return diag[l] * v - coupling[l] * beside(v)

    v0 = inv_diag[0] * f0
    t = f0 - operator(0, v0)
    rows = select((iota((H1, PH0), 1) - HR // 4) >> 1 == iota((H1, PH0), 0), 0.5)
    cols = select((iota((PW0, W1), 0) - HC // 4) >> 1 == iota((PW0, W1), 1))
    own_rows = pl.ds(pl.multiple_of(slab * H1, 8), H1)
    rhs1[own_rows, W1 : 2 * W1] = dot_right(dot_left(rows, t), cols)

    def gather_copy(dc, i):
        return pltpu.make_async_remote_copy(
            src_ref=rhs1.at[own_rows, pl.ds(W1, W1)],
            dst_ref=rhs1.at[own_rows, pl.ds(W1 - dc * W1, W1)],
            send_sem=gsend_sem.at[dc + 1, i],
            recv_sem=grecv_sem.at[dc + 1, i],
            device_id=device((slab + i) % n_slab, lin + dc),
            device_id_type=MESH,
        )

    def gather(action):
        for dc in (-1, 0, 1):
            for_recv = action == "wait_recv"

            @pl.when(exists(0, -dc if for_recv else dc))
            def _():
                for i in range(0 if dc else 1, n_slab):
                    getattr(gather_copy(dc, i), action)()

    gather("start")

    squares = []

    def emit_ar(j, x, y):
        put(3, j, y)
        squares.append((fold(x * x), fold(x * y), fold(y * y)))

    apply_a(1, emit_ar)
    halo_start(3)

    gather("wait_recv")

    def level_shape(l):
        return (H1 * n_slab) >> (l - 1), lanes((3 * W1) >> (l - 1))

    def inside(l):
        shape = level_shape(l)
        width = W1 >> (l - 1)
        j = iota(shape, 1)
        column = j + (lin - 1) * width
        return (j < 3 * width) & (column >= 0) & (column < width * n_lin)

    def level(l, f):
        mask = inside(l)
        scale = inv_diag[l]
        v = scale * f
        if l == LEVELS - 1:
            for _ in range(COARSE_SWEEPS - 1):
                v = jnp.where(mask, v + scale * (f - operator(l, v)), 0.0)
            return v
        t = jnp.where(mask, f - operator(l, v), 0.0)
        (h, w), (hn, wn) = level_shape(l), level_shape(l + 1)
        down = select((iota((hn, h), 1) >> 1) == iota((hn, h), 0), 0.5)
        across = select((iota((w, wn), 0) >> 1) == iota((w, wn), 1))
        lower = level(l + 1, dot_right(dot_left(down, t), across))
        up = select((iota((h, hn), 0) >> 1) == iota((h, hn), 1))
        back = select((iota((wn, w), 1) >> 1) == iota((wn, w), 0))
        v = v + dot_left(up, dot_right(lower, back))
        return jnp.where(mask, v + scale * (f - operator(l, v)), 0.0)

    v1 = level(1, rhs1[...])
    R1, C1 = level_shape(1)
    up = select(((iota((PH0, R1), 0) + (slab * H0 - HR // 4)) >> 1) == iota((PH0, R1), 1))
    back = select(((iota((C1, PW0), 1) - HC // 4) >> 1) + W1 == iota((C1, PW0), 0))
    v0 = v0 + dot_right(dot_left(up, v1), back)
    v0 = v0 + inv_diag[0] * (f0 - operator(0, v0))
    i, j = iota((PH0, PW0), 0), iota((PH0, PW0), 1)
    own = (i >= HR // 4) & (i < HR // 4 + H0) & (j >= HC // 4) & (j < HC // 4 + W0)
    v0 = jnp.where(own, v0, 0.0)

    c = RELAX / (1.0 + damp)
    rr = functools.reduce(jnp.add, [s[0] for s in squares])
    ra = functools.reduce(jnp.add, [s[1] for s in squares])
    aa = functools.reduce(jnp.add, [s[2] for s in squares])
    reduce_start(
        1, 3.0 * c * rr - 3.0 * c * c * ra + c * c * c * aa + 4.0 * fold(f0 * v0)
    )

    up4 = select(((iota((H, PH0), 0) + HR) >> 2) == iota((H, PH0), 1))
    v0_hi, v0_lo = split(v0)
    wide_hi = dot(up4, v0_hi).astype(BF16)
    wide_lo = dot(up4, v0_lo).astype(BF16)

    halo_arrive(3)

    def emit_pre(j, x, y):
        cols = slice(BLK * j, BLK * j + BLK)
        r = fields[1, HR : HR + H, HC + BLK * j : HC + BLK * j + BLK]
        coarse = dot(wide_hi, spread4[:, cols]) + dot(wide_lo, spread4[:, cols])
        pre_buf[:, cols] = 3.0 * c * r - 3.0 * c * c * x + c * c * c * y + coarse

    apply_a(3, emit_pre)
    pre_copy = pltpu.make_async_copy(pre_buf, pre_out, out_sem.at[2])
    pre_copy.start()
    energy = reduce_end(1)
    alpha_out[...] = alpha
    energy_out[...] = energy

    halo_sent(0, dir_in)
    halo_sent(1, res_in)
    halo_sent(2)
    halo_sent(3)
    gather("wait_send")
    for e in range(2):
        each(lambda i: part_copy(e, i, me).wait_send())
    res_copy.wait()
    pre_copy.wait()


def finish(
    sol_in,
    res_in,
    pre_in,
    dir_in,
    alpha,
    energy,
    rho,
    sol_out,
    res_out,
    pre_out,
    ndir_out,
    total_out,
    sol,
    res,
    pre,
    direction,
    ndir,
    load_sem,
    store_sem,
):
    pairs = ((dir_in, direction), (sol_in, sol), (res_in, res), (pre_in, pre))
    loads = [pltpu.make_async_copy(a, b, load_sem.at[i]) for i, (a, b) in enumerate(pairs)]
    pairs = ((sol, sol_out), (res, res_out), (pre, pre_out), (ndir, ndir_out))
    stores = [pltpu.make_async_copy(a, b, store_sem.at[i]) for i, (a, b) in enumerate(pairs)]
    for load in loads:
        load.start()
    total_out[0] = energy[0, 0]
    beta = jnp.full((1, 1), energy[0, 0], F32) / jnp.full((1, 1), rho[0], F32)
    loads[0].wait()
    loads[1].wait()
    sol[...] = sol[...] + alpha[0, 0] * direction[...]
    stores[0].start()
    loads[2].wait()
    stores[1].start()
    loads[3].wait()
    stores[2].start()
    ndir[...] = pre[...] + beta * direction[...]
    stores[3].start()
    for store in stores:
        store.wait()


def solution(mesh):
    n_grp, n_slab, n_col = (mesh.shape[a] for a in ("grp", "slab", "col"))
    n_lin = n_grp * n_col

    def on_device(sol, res, direction, row_taps, col_taps, damping, rho, diag, coupling):
        H, W = sol.shape
        taps = row_taps.shape[0]
        PH, PW = H + 2 * HR, W + 2 * HC
        WIN = BLK + 2 * HC
        any_spec = pl.BlockSpec(memory_space=pl.ANY)
        smem = pl.BlockSpec(memory_space=pltpu.SMEM)
        vmem = pl.BlockSpec(memory_space=pltpu.VMEM)
        tile = jax.ShapeDtypeStruct((H, W), F32)
        dma = pltpu.SemaphoreType.DMA
        rho = rho.reshape(1)
        new_res, pre, alpha, energy = pl.pallas_call(
            functools.partial(kernel, (H, W, n_slab, n_grp, n_col, taps)),
            out_shape=[tile] * 2 + [jax.ShapeDtypeStruct((1, 1), F32)] * 2,
            in_specs=[any_spec] * 2 + [smem] * 6,
            out_specs=[any_spec] * 2 + [vmem] * 2,
            scratch_shapes=[
                pltpu.VMEM((4, PH, PW), F32),
                pltpu.VMEM((WIN, WIN), F32),
                pltpu.VMEM((3, WIN, BLK), BF16),
                pltpu.VMEM((3, WIN, BLK), BF16),
                pltpu.VMEM((H, PH), BF16),
                pltpu.VMEM((H, PH), BF16),
                pltpu.VMEM((H, PW), BF16),
                pltpu.VMEM((H, PW), BF16),
                pltpu.VMEM((PW, lanes(PW // 4)), BF16),
                pltpu.VMEM((lanes(PW // 4), W), BF16),
                pltpu.VMEM((H, W), F32),
                pltpu.VMEM((H // 8 * n_slab, 3 * (W // 8)), F32),
                pltpu.VMEM((2, n_slab * n_lin, 1, 128), F32),
                dma((3,)),
                dma((4,)),
                dma((4, 8)),
                dma((4, 8)),
                dma((3, n_slab)),
                dma((3, n_slab)),
                dma((2, n_slab * n_lin)),
                dma((2, n_slab * n_lin)),
            ],
            compiler_params=pltpu.CompilerParams(
                collective_id=0, has_side_effects=True, vmem_limit_bytes=60 * 1024 * 1024
            ),
        )(
            res,
            direction,
            row_taps,
            col_taps,
            damping.reshape(1),
            rho,
            diag,
            coupling,
        )
        outs = pl.pallas_call(
            finish,
            out_shape=[tile] * 4 + [jax.ShapeDtypeStruct((1,), F32)],
            in_specs=[any_spec] * 4 + [smem] * 3,
            out_specs=[any_spec] * 4 + [smem],
            scratch_shapes=[pltpu.VMEM((H, W), F32)] * 5 + [dma((4,)), dma((4,))],
            compiler_params=pltpu.CompilerParams(vmem_limit_bytes=60 * 1024 * 1024),
        )(sol, new_res, pre, direction, alpha, energy, rho)
        return (*outs[:4], outs[4].reshape(()))

    tile = P("slab", ("grp", "col"))
    return jax.shard_map(
        on_device,
        mesh=mesh,
        in_specs=(tile, tile, tile, P(), P(), P(), P(), P(), P()),
        out_specs=(tile, tile, tile, tile, P()),
        check_vma=False,
    )
```

```python
import functools

import jax
import jax.numpy as jnp
from jax import lax
from jax.experimental import pallas as pl
from jax.experimental.pallas import tpu as pltpu
from jax.sharding import PartitionSpec as P

SWEEPS = 3
LEVELS = 4
COARSE_SWEEPS = 4
RELAX = 2.0 / 3.0
HR = 32
HC = 128
BLK = 256
MESH = pl.DeviceIdType.MESH
F32 = jnp.float32
BF16 = jnp.bfloat16
DIRS = [(0, -1), (0, 1), (-1, 0), (1, 0), (-1, -1), (-1, 1), (1, -1), (1, 1)]


def split(x):
    hi = x.astype(BF16)
    return hi, (x - hi.astype(F32)).astype(BF16)


def dot(a, b):
    return jnp.dot(a, b, preferred_element_type=F32)


def dot_left(sel, x):
    hi, lo = split(x)
    return dot(sel, hi) + dot(sel, lo)


def dot_right(x, sel):
    hi, lo = split(x)
    return dot(hi, sel) + dot(lo, sel)


def iota(shape, dim):
    return lax.broadcasted_iota(jnp.int32, shape, dim)


def select(condition, value=1.0):
    return jnp.where(condition, F32(value), F32(0.0)).astype(BF16)


def lanes(n):
    return -(-n // 128) * 128


def fold(x):
    rows, cols = x.shape
    total = x.reshape(rows // 8, 8, cols).sum(axis=0)
    out = total[:, :128]
    for b in range(1, cols // 128):
        out = out + total[:, 128 * b : 128 * b + 128]
    return out


def beside(v):
    rows, cols = v.shape
    i = iota(v.shape, 0)
    up = jnp.where(i == 0, 0.0, pltpu.roll(v, 1, 0))
    down = jnp.where(i == rows - 1, 0.0, pltpu.roll(v, rows - 1, 0))
    return up + down + pltpu.roll(v, 1, 1) + pltpu.roll(v, cols - 1, 1)


def kernel(
    sizes,
    res_in,
    dir_in,
    row_taps,
    col_taps,
    damping,
    rho,
    diag,
    coupling,
    res_out,
    pre_out,
    alpha_out,
    energy_out,
    fields,
    packed,
    arrived,
    band,
    mc_hi,
    mc_lo,
    mr_hi,
    mr_lo,
    t_hi,
    t_lo,
    sum4,
    spread4,
    pre_buf,
    rhs1,
    parts_in,
    local_sem,
    out_sem,
    send_sem,
    recv_sem,
    gsend_sem,
    grecv_sem,
    psend_sem,
    precv_sem,
):
    H, W, n_slab, n_grp, n_col, taps = sizes
    n_lin = n_grp * n_col
    reach = taps // 2
    PH, PW = H + 2 * HR, W + 2 * HC
    slab = lax.axis_index("slab")
    lin = lax.axis_index("grp") * n_col + lax.axis_index("col")

    grp, col = lax.axis_index("grp"), lax.axis_index("col")
    at = {0: (grp, col)}
    for dc in (-1, 1):
        l = lin + dc + n_lin
        at[dc] = (lax.rem(lax.div(l, n_col), n_grp), lax.rem(l, n_col))
    grps = [lax.rem(grp + i, n_grp) for i in range(n_grp)]
    slabs = [lax.rem(slab + i, n_slab) for i in range(n_slab)]
    cols_of = [lax.rem(col + i, n_col) for i in range(n_col)]

    def beside_device(s, dc):
        return (at[dc][0], s, at[dc][1])

    def exists(dz, dc):
        s, l = slab + dz, lin + dc
        return (s >= 0) & (s < n_slab) & (l >= 0) & (l < n_lin)

    centre = (pl.ds(HR, H), pl.ds(HC, W))

    loads = [
        pltpu.make_async_copy(dir_in, fields.at[0].at[centre], local_sem.at[0]),
        pltpu.make_async_copy(res_in, fields.at[1].at[centre], local_sem.at[1]),
    ]
    for load in loads:
        load.start()

    barrier = pltpu.get_barrier_semaphore()
    count = n_slab * n_lin
    me = slab * n_lin + lin

    few = count <= 64

    def other(i):
        if few:
            return (
                grps[i // (n_slab * n_col)],
                slabs[i // n_col % n_slab],
                cols_of[i % n_col],
            )
        g = lax.div(i, n_slab * n_col)
        rest = lax.rem(i, n_slab * n_col)
        return (
            lax.rem(grp + g, n_grp),
            lax.rem(slab + lax.div(rest, n_col), n_slab),
            lax.rem(col + lax.rem(rest, n_col), n_col),
        )

    def each(action):
        if few:
            for i in reversed(range(1, count)):
                action(i)
            return

        def step(i, carry):
            action(i)
            return carry

        lax.fori_loop(1, count, step, 0)

    each(
        lambda i: pl.semaphore_signal(
            barrier, inc=1, device_id=other(i), device_id_type=MESH
        )
    )

    def side(d, halo, extent):
        return {-1: (0, halo), 0: (halo, extent), 1: (halo + extent, halo)}[d]

    for f in range(4):
        for c0 in (0, HC + W):
            fields[f, :, c0 : c0 + HC] = jnp.zeros((PH, HC), F32)
    for dz in (-1, 1):
        r0 = side(dz, HR, H)[0]

        @pl.when(jnp.logical_not(exists(dz, 0)))
        def _():
            for f in range(4):
                fields[f, r0 : r0 + HR, HC : HC + W] = jnp.zeros((HR, W), F32)

    W1 = W // 8
    H1 = H // 8
    for dc, c0 in ((-1, 0), (1, 2 * W1)):

        @pl.when(jnp.logical_not(exists(0, dc)))
        def _():
            rhs1[:, c0 : c0 + W1] = jnp.zeros((H1 * n_slab, W1), F32)

    pl.semaphore_wait(barrier, count - 1)

    SIDE, CORNER = H // 4, HR // 4
    EDGE = HC // 4
    TOP, BOTTOM = slice(SIDE, SIDE + CORNER), slice(SIDE + CORNER, SIDE + 2 * CORNER)

    def pack(f):
        for i, c0 in enumerate((HC, HC + W - 128)):
            first = 0 if i == 0 else 128 - EDGE
            x = fields[f, HR : HR + H, c0 : c0 + 128][:, first : first + EDGE]

            def groups(low, n):
                return jnp.concatenate([x[low + n * g : low + n * g + n] for g in range(4)], axis=1)

            packed[f, i, 0:SIDE] = groups(0, SIDE)
            packed[f, i, TOP] = groups(0, CORNER)
            packed[f, i, BOTTOM] = groups(H - HR, CORNER)

    def unpack(f):
        for i, c0 in enumerate((HC - EDGE, HC + W)):
            dc = 2 * i - 1
            for dz, r0, part, n in (
                (0, HR, slice(0, SIDE), SIDE),
                (-1, 0, TOP, CORNER),
                (1, HR + H, BOTTOM, CORNER),
            ):

                @pl.when(exists(dz, dc))
                def _():
                    x = arrived[f, i, part]
                    for g in range(4):
                        fields[f, r0 + n * g : r0 + n * g + n, c0 : c0 + EDGE] = x[
                            :, EDGE * g : EDGE * g + EDGE
                        ]

    def halo_copy(f, source, k):
        dz, dc = DIRS[k]
        if dc == 0:
            rs = 0 if dz < 0 else H - HR
            rd = HR + H if dz < 0 else 0
            if source is None:
                src = fields.at[f, pl.ds(HR + rs, HR), pl.ds(HC, W)]
            else:
                src = source.at[pl.ds(rs, HR), pl.ds(0, W)]
            dst = fields.at[f, pl.ds(rd, HR), pl.ds(HC, W)]
        else:
            i = 0 if dc < 0 else 1
            low, n = {0: (0, SIDE), -1: (SIDE, CORNER), 1: (SIDE + CORNER, CORNER)}[dz]
            land = {0: 0, -1: SIDE + CORNER, 1: SIDE}[dz]
            src = packed.at[f, i, pl.ds(low, n)]
            dst = arrived.at[f, 1 - i, pl.ds(land, n)]
        return pltpu.make_async_remote_copy(
            src_ref=src,
            dst_ref=dst,
            send_sem=send_sem.at[f, k],
            recv_sem=recv_sem.at[f, k],
            device_id=beside_device(slab + dz, dc),
            device_id_type=MESH,
        )

    def halo_start(f, source=None, load=None):
        def start(rows):
            for k, (dz, dc) in enumerate(DIRS):
                if (dc == 0) == rows:

                    @pl.when(exists(dz, dc))
                    def _():
                        halo_copy(f, source, k).start()

        start(True)
        if load is not None:
            load.wait()
        pack(f)
        start(False)

    def halo_arrive(f, source=None):
        for k, (dz, dc) in enumerate(DIRS):

            @pl.when(exists(-dz, -dc))
            def _():
                halo_copy(f, source, k).wait_recv()

        unpack(f)

    def halo_sent(f, source=None):
        for k, (dz, dc) in enumerate(DIRS):

            @pl.when(exists(dz, dc))
            def _():
                halo_copy(f, source, k).wait_send()

    halo_start(0, dir_in, loads[0])
    halo_start(1, res_in, loads[1])

    def banded(ref, first, rows, cols, offset):
        total = ref[0]
        for a in range(1, taps):
            total = total + ref[a]
        inverse = 1.0 / jnp.full((1, 1), total, F32)
        gap = iota((rows, cols), 1) - iota((rows, cols), 0) + (reach + offset - first)
        out = jnp.zeros((rows, cols), F32)
        for a in range(taps):
            out = jnp.where(gap == a, ref[a], out)
        return out * inverse

    def gram(c, keep):
        hi, lo = split(c)
        khi, klo = hi[:, keep], lo[:, keep]
        hit, lot = hi.T, lo.T
        return dot(hit, khi) + dot(lot, khi) + dot(hit, klo)

    for r in range(0, PH, 32):
        band[r : r + 32, 0:PH] = banded(row_taps, r, 32, PH, 0)
    m = iota((PH, PH), 0) + (slab * H - HR)
    c = jnp.where((m >= 0) & (m < H * n_slab), band[0:PH, 0:PH], 0.0)
    hi, lo = split(c)
    hit, lot = hi.T[HR : HR + H], lo.T[HR : HR + H]
    g = dot(hit, hi) + dot(lot, hi) + dot(hit, lo)
    ghi, glo = split(g)
    mr_hi[...] = ghi
    mr_lo[...] = glo

    WIN = BLK + 2 * HC
    band[...] = jnp.zeros((WIN, WIN), F32)
    for r in range(0, 128, 32):
        strip = banded(col_taps, r, 32, 384, -128)
        for b in range(WIN // 128):
            low = max(b - 1, 0)
            high = min(b + 2, WIN // 128)
            band[128 * b + r : 128 * b + r + 32, 128 * low : 128 * high] = strip[
                :, 128 * (low - b + 1) : 128 * (high - b + 1)
            ]
    blocks = W // BLK
    for v, j in ((0, 0), (1, None), (2, blocks - 1)):
        c = band[...]
        if j is not None:
            m = iota((WIN, WIN), 0) + (lin * W + BLK * j - HC)
            c = jnp.where((m >= 0) & (m < W * n_lin), c, 0.0)
        ghi, glo = split(gram(c, slice(HC, HC + BLK)))
        mc_hi[v] = ghi
        mc_lo[v] = glo

    H0, W0 = H // 4, W // 4
    PH0, PW0 = PH // 4, lanes(PW // 4)
    sum4[...] = select((iota((PW, PW0), 0) >> 2) == iota((PW, PW0), 1), 0.25)
    spread4[...] = select(
        ((iota((PW0, W), 1) + HC) >> 2) == iota((PW0, W), 0)
    )

    damp = jnp.full((1, 1), damping[0], F32)

    def apply_a(f, emit):
        for j in range(PW // BLK):
            cols = slice(BLK * j, BLK * j + BLK)
            xh, xl = split(fields[f, :, cols])
            t = dot(mr_hi[...], xh) + dot(mr_hi[...], xl) + dot(mr_lo[...], xh)
            th, tl = split(t)
            t_hi[:, cols] = th
            t_lo[:, cols] = tl
        for j in range(blocks):
            v = 0 if j == 0 else (2 if j == blocks - 1 else 1)
            win = slice(BLK * j, BLK * j + WIN)
            th, tl = t_hi[:, win], t_lo[:, win]
            mh, ml = mc_hi[v], mc_lo[v]
            x = fields[f, HR : HR + H, HC + BLK * j : HC + BLK * j + BLK]
            emit(j, x, dot(th, mh) + dot(tl, mh) + dot(th, ml) + damp * x)

    def put(f, j, value):
        fields[f, HR : HR + H, HC + BLK * j : HC + BLK * j + BLK] = value

    def part_copy(e, i, slot):
        return pltpu.make_async_remote_copy(
            src_ref=parts_in.at[e, me],
            dst_ref=parts_in.at[e, slot],
            send_sem=psend_sem.at[e, i],
            recv_sem=precv_sem.at[e, i],
            device_id=other(i),
            device_id_type=MESH,
        )

    def reduce_start(e, value):
        parts_in[e, me] = jnp.sum(value, axis=0, keepdims=True)
        each(lambda i: part_copy(e, i, me).start())

    def reduce_end(e):
        each(lambda i: part_copy(e, i, me).wait_recv())
        return jnp.sum(jnp.sum(parts_in[e], axis=0), axis=1, keepdims=True)

    halo_arrive(0, dir_in)
    parts = []

    def emit_q(j, x, y):
        put(2, j, y)
        parts.append(fold(x * y))

    apply_a(0, emit_q)
    reduce_start(0, functools.reduce(jnp.add, parts))
    halo_start(2)
    halo_arrive(1, res_in)
    halo_arrive(2)
    rho_v = jnp.full((1, 1), rho[0], F32)
    alpha = rho_v / reduce_end(0)

    pick_rows = select((iota((PH0, PH), 1) >> 2) == iota((PH0, PH), 0))
    f0 = jnp.zeros((PH0, PW0), F32)
    for j in range(PW // BLK):
        cols = slice(BLK * j, BLK * j + BLK)
        r = fields[1, :, cols] - alpha * fields[2, :, cols]
        fields[1, :, cols] = r
        f0 = f0 + dot_right(dot_left(pick_rows, r), sum4[cols, :])
    res_copy = pltpu.make_async_copy(fields.at[1].at[centre], res_out, out_sem.at[0])
    res_copy.start()

    inv_diag = [RELAX / jnp.full((1, 1), diag[l], F32) for l in range(LEVELS)]

    def operator(l, v):
        return diag[l] * v - coupling[l] * beside(v)

    v0 = inv_diag[0] * f0
    t = f0 - operator(0, v0)
    rows = select((iota((H1, PH0), 1) - HR // 4) >> 1 == iota((H1, PH0), 0), 0.5)
    cols = select((iota((PW0, W1), 0) - HC // 4) >> 1 == iota((PW0, W1), 1))
    own_rows = pl.ds(pl.multiple_of(slab * H1, 8), H1)
    rhs1[own_rows, W1 : 2 * W1] = dot_right(dot_left(rows, t), cols)

    def gather_copy(dc, i):
        return pltpu.make_async_remote_copy(
            src_ref=rhs1.at[own_rows, pl.ds(W1, W1)],
            dst_ref=rhs1.at[own_rows, pl.ds(W1 - dc * W1, W1)],
            send_sem=gsend_sem.at[dc + 1, i],
            recv_sem=grecv_sem.at[dc + 1, i],
            device_id=beside_device(slabs[i], dc),
            device_id_type=MESH,
        )

    def gather(action):
        for dc in (-1, 0, 1):
            for_recv = action == "wait_recv"

            @pl.when(exists(0, -dc if for_recv else dc))
            def _():
                for i in range(0 if dc else 1, n_slab):
                    getattr(gather_copy(dc, i), action)()

    gather("start")

    squares = []

    def emit_ar(j, x, y):
        put(3, j, y)
        squares.append((fold(x * x), fold(x * y), fold(y * y)))

    apply_a(1, emit_ar)
    halo_start(3)

    gather("wait_recv")

    def level_shape(l):
        return (H1 * n_slab) >> (l - 1), lanes((3 * W1) >> (l - 1))

    def inside(l):
        shape = level_shape(l)
        width = W1 >> (l - 1)
        j = iota(shape, 1)
        column = j + (lin - 1) * width
        return (j < 3 * width) & (column >= 0) & (column < width * n_lin)

    def level(l, f):
        mask = inside(l)
        scale = inv_diag[l]
        v = scale * f
        if l == LEVELS - 1:
            for _ in range(COARSE_SWEEPS - 1):
                v = jnp.where(mask, v + scale * (f - operator(l, v)), 0.0)
            return v
        t = jnp.where(mask, f - operator(l, v), 0.0)
        (h, w), (hn, wn) = level_shape(l), level_shape(l + 1)
        down = select((iota((hn, h), 1) >> 1) == iota((hn, h), 0), 0.5)
        across = select((iota((w, wn), 0) >> 1) == iota((w, wn), 1))
        lower = level(l + 1, dot_right(dot_left(down, t), across))
        up = select((iota((h, hn), 0) >> 1) == iota((h, hn), 1))
        back = select((iota((wn, w), 1) >> 1) == iota((wn, w), 0))
        v = v + dot_left(up, dot_right(lower, back))
        return jnp.where(mask, v + scale * (f - operator(l, v)), 0.0)

    v1 = level(1, rhs1[...])
    R1, C1 = level_shape(1)
    up = select(((iota((PH0, R1), 0) + (slab * H0 - HR // 4)) >> 1) == iota((PH0, R1), 1))
    back = select(((iota((C1, PW0), 1) - HC // 4) >> 1) + W1 == iota((C1, PW0), 0))
    v0 = v0 + dot_right(dot_left(up, v1), back)
    v0 = v0 + inv_diag[0] * (f0 - operator(0, v0))
    i, j = iota((PH0, PW0), 0), iota((PH0, PW0), 1)
    own = (i >= HR // 4) & (i < HR // 4 + H0) & (j >= HC // 4) & (j < HC // 4 + W0)
    v0 = jnp.where(own, v0, 0.0)

    c = RELAX / (1.0 + damp)
    rr = functools.reduce(jnp.add, [s[0] for s in squares])
    ra = functools.reduce(jnp.add, [s[1] for s in squares])
    aa = functools.reduce(jnp.add, [s[2] for s in squares])
    reduce_start(
        1, 3.0 * c * rr - 3.0 * c * c * ra + c * c * c * aa + 4.0 * fold(f0 * v0)
    )

    up4 = select(((iota((H, PH0), 0) + HR) >> 2) == iota((H, PH0), 1))
    v0_hi, v0_lo = split(v0)
    wide_hi = dot(up4, v0_hi).astype(BF16)
    wide_lo = dot(up4, v0_lo).astype(BF16)

    halo_arrive(3)

    def emit_pre(j, x, y):
        cols = slice(BLK * j, BLK * j + BLK)
        r = fields[1, HR : HR + H, HC + BLK * j : HC + BLK * j + BLK]
        coarse = dot(wide_hi, spread4[:, cols]) + dot(wide_lo, spread4[:, cols])
        pre_buf[:, cols] = 3.0 * c * r - 3.0 * c * c * x + c * c * c * y + coarse

    apply_a(3, emit_pre)
    pre_copy = pltpu.make_async_copy(pre_buf, pre_out, out_sem.at[2])
    pre_copy.start()
    energy = reduce_end(1)
    alpha_out[...] = alpha
    energy_out[...] = energy

    halo_sent(0, dir_in)
    halo_sent(1, res_in)
    halo_sent(2)
    halo_sent(3)
    gather("wait_send")
    for e in range(2):
        each(lambda i: part_copy(e, i, me).wait_send())
    res_copy.wait()
    pre_copy.wait()


def finish(
    sol_in,
    res_in,
    pre_in,
    dir_in,
    alpha,
    energy,
    rho,
    sol_out,
    res_out,
    pre_out,
    ndir_out,
    total_out,
    sol,
    res,
    pre,
    direction,
    ndir,
    load_sem,
    store_sem,
):
    pairs = ((dir_in, direction), (sol_in, sol), (res_in, res), (pre_in, pre))
    loads = [pltpu.make_async_copy(a, b, load_sem.at[i]) for i, (a, b) in enumerate(pairs)]
    pairs = ((sol, sol_out), (res, res_out), (pre, pre_out), (ndir, ndir_out))
    stores = [pltpu.make_async_copy(a, b, store_sem.at[i]) for i, (a, b) in enumerate(pairs)]
    for load in loads:
        load.start()
    total_out[0] = energy[0, 0]
    beta = jnp.full((1, 1), energy[0, 0], F32) / jnp.full((1, 1), rho[0], F32)
    loads[0].wait()
    loads[1].wait()
    sol[...] = sol[...] + alpha[0, 0] * direction[...]
    stores[0].start()
    loads[2].wait()
    stores[1].start()
    loads[3].wait()
    stores[2].start()
    ndir[...] = pre[...] + beta * direction[...]
    stores[3].start()
    for store in stores:
        store.wait()


def solution(mesh):
    n_grp, n_slab, n_col = (mesh.shape[a] for a in ("grp", "slab", "col"))
    n_lin = n_grp * n_col

    def on_device(sol, res, direction, row_taps, col_taps, damping, rho, diag, coupling):
        H, W = sol.shape
        taps = row_taps.shape[0]
        PH, PW = H + 2 * HR, W + 2 * HC
        WIN = BLK + 2 * HC
        any_spec = pl.BlockSpec(memory_space=pl.ANY)
        smem = pl.BlockSpec(memory_space=pltpu.SMEM)
        vmem = pl.BlockSpec(memory_space=pltpu.VMEM)
        tile = jax.ShapeDtypeStruct((H, W), F32)
        dma = pltpu.SemaphoreType.DMA
        rho = rho.reshape(1)
        new_res, pre, alpha, energy = pl.pallas_call(
            functools.partial(kernel, (H, W, n_slab, n_grp, n_col, taps)),
            out_shape=[tile] * 2 + [jax.ShapeDtypeStruct((1, 1), F32)] * 2,
            in_specs=[any_spec] * 2 + [smem] * 6,
            out_specs=[any_spec] * 2 + [vmem] * 2,
            scratch_shapes=[
                pltpu.VMEM((4, PH, PW), F32),
                pltpu.VMEM((4, 2, H // 4 + HR // 2, 128), F32),
                pltpu.VMEM((4, 2, H // 4 + HR // 2, 128), F32),
                pltpu.VMEM((WIN, WIN), F32),
                pltpu.VMEM((3, WIN, BLK), BF16),
                pltpu.VMEM((3, WIN, BLK), BF16),
                pltpu.VMEM((H, PH), BF16),
                pltpu.VMEM((H, PH), BF16),
                pltpu.VMEM((H, PW), BF16),
                pltpu.VMEM((H, PW), BF16),
                pltpu.VMEM((PW, lanes(PW // 4)), BF16),
                pltpu.VMEM((lanes(PW // 4), W), BF16),
                pltpu.VMEM((H, W), F32),
                pltpu.VMEM((H // 8 * n_slab, 3 * (W // 8)), F32),
                pltpu.VMEM((2, n_slab * n_lin, 1, 128), F32),
                dma((3,)),
                dma((4,)),
                dma((4, 8)),
                dma((4, 8)),
                dma((3, n_slab)),
                dma((3, n_slab)),
                dma((2, n_slab * n_lin)),
                dma((2, n_slab * n_lin)),
            ],
            compiler_params=pltpu.CompilerParams(
                collective_id=0, has_side_effects=True, vmem_limit_bytes=60 * 1024 * 1024
            ),
        )(
            res,
            direction,
            row_taps,
            col_taps,
            damping.reshape(1),
            rho,
            diag,
            coupling,
        )
        outs = pl.pallas_call(
            finish,
            out_shape=[tile] * 4 + [jax.ShapeDtypeStruct((1,), F32)],
            in_specs=[any_spec] * 4 + [smem] * 3,
            out_specs=[any_spec] * 4 + [smem],
            scratch_shapes=[pltpu.VMEM((H, W), F32)] * 5 + [dma((4,)), dma((4,))],
            compiler_params=pltpu.CompilerParams(vmem_limit_bytes=60 * 1024 * 1024),
        )(sol, new_res, pre, direction, alpha, energy, rho)
        return (*outs[:4], outs[4].reshape(()))

    tile = P("slab", ("grp", "col"))
    return jax.shard_map(
        on_device,
        mesh=mesh,
        in_specs=(tile, tile, tile, P(), P(), P(), P(), P(), P()),
        out_specs=(tile, tile, tile, tile, P()),
        check_vma=False,
    )
```
